32 devices in a mesh: group: 2 (over y), dp: 4 (over z), section: 2 (over x), mp: 2 (over core).
Axes of the slice: x: 2, y: 2, z: 4, core: 2. Of those that a mesh axis runs over, the one named last changes fastest.
Arguments:
- acts: bfloat16 [2, 1024, 8192], P('section', ('group', 'dp'), 'mp'), parts along dimension 1, may hold values from -7 to 7
- cotangent: bfloat16 [1024, 8192], P(('group', 'dp'), 'mp'), parts along dimension 0, may hold values from -7 to 7
- in_weight: bfloat16 [2, 512, 8192], P('section', 'dp', 'mp'), may hold values from -0.25 to 0.25
- out_weight: bfloat16 [2, 512, 8192], P('section', 'dp', 'mp'), may hold values from -0.0625 to 0.0625
- in_factor: bfloat16 [2, 64, 8192], P('section', None, 'mp'), may hold values from -0.0625 to 0.0625
- out_factor: bfloat16 [2, 64, 512], P('section'), may hold values from -0.25 to 0.25
- damping: float32 [2], P('section'), may hold values from 0.25 to 4
- lengths: int32 [8, 4], P(('group', 'dp')), parts along dimension 0, may hold values from 1 to 64, 128 in all within a row
Outputs:
- adjoints: bfloat16 [2, 1024, 8192], P('section', ('group', 'dp'), 'mp'), parts along dimension 1
- leverage: float32 [2, 32], P('section', ('group', 'dp')), parts along dimension 1
The draws below stay inside these ranges and needn't reach their ends.
There are 2 independent parts, one for each index of `group`. The reference program is written for one: setup_inputs(seed, part) draws one part's arguments, and reference() takes and returns one part's arrays. A program takes and returns all parts, laid end to end along the dimension named above; an argument that names none is the same for every part. Nothing has to cross between parts.
Inputs may be any that keep to these rules, and one draw needn't show every extreme that they name: `lengths`: each row sums to 128, and its largest entry is exactly 64.
All inputs are finite; a program needn't handle non-finite values.
Results may differ from the reference program's by a relative error of at most 0.0054.
Values may be sent and summed in bfloat16 or wider, within the bound.
No kernel may reach another device: no remote copies, remote signals or barrier semaphores. Data moves between devices by JAX's collectives and lax.ppermute only.
A program may use at most 64 MiB of HBM per device.

```python
import math
import jax
import jax.numpy as jnp
import numpy as np
from jax import lax

D = 8192
R = 512
KIN = 64
KOUT = 64
TOK_DEV = 128
EX_DEV = 4
TOKENS = 512
N_DP = 4
N_SECTION = 2


def shared_rows(key, lead, blocks, width, whole_scale, block_scale):
    key_whole, key_block = jax.random.split(key)
    whole = jax.random.normal(key_whole, (lead, 1, width), jnp.float32) * whole_scale
    block = jax.random.normal(key_block, (lead, blocks, width), jnp.float32) * block_scale
    return whole + block


def token_field(key, lead):
    blocks = TOKENS // TOK_DEV
    key_noise, key_shared = jax.random.split(key)
    noise = jax.random.truncated_normal(key_noise, -6.0, 6.0, (lead, blocks, TOK_DEV, D), jnp.float32)
    shared = shared_rows(key_shared, lead, blocks, D, 0.47, 0.18)
    total = noise + shared[:, :, None, :]
    return jnp.clip(total, -7.0, 7.0)


def draw_acts(key, part):
    field = token_field(jax.random.fold_in(key, 11), N_SECTION)
    return field.reshape(N_SECTION, TOKENS, D).astype(jnp.bfloat16)


def draw_cotangent(key, part):
    field = token_field(jax.random.fold_in(key, 23), 1)
    return field.reshape(TOKENS, D).astype(jnp.bfloat16)


def level_of(own_key, dims, pieces, smallest, high):
    def one(axis_at, parts):
        steps = jax.random.uniform(jax.random.fold_in(jax.random.fold_in(own_key, 6), axis_at), (parts,), jnp.float32, smallest / len(pieces), high / len(pieces))
        return jnp.repeat(jnp.exp(steps), dims[axis_at] // parts).reshape((-1,) + (1,) * (len(dims) - axis_at - 1))

    factor_of = one(*pieces[0])
    for cut in pieces[1:]:
        factor_of = factor_of * one(*cut)
    return factor_of


def split_up(count, total, most, lean):
    weights = [(1 << 20) // math.isqrt(standing ** lean) + 1 for standing in range(2, count + 1)]
    rest, holding = total - most - (count - 1), [1] * (count - 1)
    while rest > 0:
        candidates = [i for i in range(count - 1) if holding[i] < most]
        pool, budget = sum([weights[i] for i in candidates]), rest
        for i in candidates:
            extra = min(most - holding[i], max(1, budget * weights[i] // pool), rest)
            holding[i] = holding[i] + extra
            rest = rest - extra
    return np.array([most] + holding)


def ragged(rng, number_of, total, reach, skew):
    if number_of == 2:
        one = jax.random.randint(rng, (), max(1, total - reach), min(reach, total - 1) + 1)
        return jnp.stack([one, total - one])
    tallies = jnp.asarray(split_up(number_of, total, reach, skew), jnp.int32)
    pairs = (number_of - 1) // 2
    donor, sink = tallies[1:1 + 2 * pairs:2], tallies[2:2 + 2 * pairs:2]
    room = jnp.minimum(donor - 1, reach - sink)
    moved = jax.random.randint(jax.random.fold_in(rng, 1), (pairs,), 0, 1 << 20) % (room + 1)
    tallies = tallies.at[1:1 + 2 * pairs:2].set(donor - moved).at[2:2 + 2 * pairs:2].set(sink + moved)
    return tallies[jax.random.permutation(jax.random.fold_in(rng, 2), number_of)]


def centred(key, dims, deviation, reach, pieces=(), kind=jnp.bfloat16):
    factor_of = level_of(key, dims, pieces, -0.22, 0.18) if pieces else 1.0
    entries = jax.random.normal(key, dims, jnp.float32) * deviation * factor_of
    return jnp.minimum(jnp.maximum(entries, -reach), reach).astype(kind)


def setup_inputs(seed: int = 0, part: int = 0) -> dict:
    key_of = jax.random.split(jax.random.key(seed), 9)
    own_keys = jax.random.split(jax.random.fold_in(key_of[8], part), 9)
    acts = draw_acts(jax.random.fold_in(jax.random.fold_in(key_of[8], part), 71), part)
    cotangent = draw_cotangent(jax.random.fold_in(jax.random.fold_in(key_of[8], part), 71), part)
    in_weight = centred(key_of[2], (N_SECTION, R, D), R ** -0.5, 0.25, ((0, 2), (1, 4), (2, 2)))
    out_weight = centred(key_of[3], (N_SECTION, R, D), D ** -0.5, 0.0625, ((0, 2), (1, 4), (2, 2)))
    in_factor = centred(key_of[4], (N_SECTION, KIN, D), D ** -0.5, 0.0625, ((0, 2), (2, 2)))
    out_factor = centred(key_of[5], (N_SECTION, KOUT, R), R ** -0.5, 0.25, ((0, 2),))
    damping = jnp.clip(jnp.exp(math.log(4.0) - 2.7725887 * jax.random.uniform(key_of[6], (N_SECTION,), jnp.float32) ** level_of(key_of[6], (N_SECTION,), ((0, 2),), -0.2, 0.2)), 0.25, 4.0)
    lengths = jax.vmap(lambda own: ragged(own, EX_DEV, TOK_DEV, TOK_DEV // 2, 2))(jax.random.split(own_keys[7], N_DP)).reshape((N_DP, EX_DEV)).astype(jnp.int32)
    return {"acts": acts, "cotangent": cotangent, "in_weight": in_weight, "out_weight": out_weight, "in_factor": in_factor, "out_factor": out_factor, "damping": damping, "lengths": lengths}


def reference(acts, cotangent, in_weight, out_weight, in_factor, out_factor, damping, lengths):
    ends = jnp.cumsum(lengths, axis=1).astype(jnp.int32)
    positions = jnp.arange(TOK_DEV, dtype=jnp.int32)
    doc_index = jnp.sum((positions[None, :, None] >= ends[:, None, :]).astype(jnp.int32), axis=2)
    member = (doc_index[:, :, None] == jnp.arange(EX_DEV, dtype=jnp.int32)[None, None, :]).astype(jnp.float32)
    adjoint_now = cotangent
    adjoint_list = [None] * N_SECTION
    score_list = [None] * N_SECTION
    columns = KIN * KOUT
    docs_all = N_DP * EX_DEV
    for section_id in reversed(range(N_SECTION)):
        rank_grad = jnp.dot(adjoint_now.astype(jnp.float32), out_weight[section_id].T.astype(jnp.float32), preferred_element_type=jnp.float32).astype(jnp.bfloat16)
        new_adjoint = (adjoint_now.astype(jnp.float32) + jnp.dot(rank_grad.astype(jnp.float32), in_weight[section_id].astype(jnp.float32), preferred_element_type=jnp.float32)).astype(jnp.bfloat16)
        out_proj = jnp.dot(rank_grad.astype(jnp.float32), out_factor[section_id].T.astype(jnp.float32), preferred_element_type=jnp.float32)
        in_proj = jnp.dot(acts[section_id].astype(jnp.float32), in_factor[section_id].T.astype(jnp.float32), preferred_element_type=jnp.float32)
        grad_rows = jnp.einsum('dte,dto,dti->deoi', member, out_proj.reshape(N_DP, TOK_DEV, KOUT), in_proj.reshape(N_DP, TOK_DEV, KIN), precision=lax.Precision.HIGHEST).reshape(docs_all, columns)
        kernel = jnp.dot(grad_rows, grad_rows.T, precision=lax.Precision.HIGHEST)
        shift_value = damping[section_id] * (columns * TOK_DEV / EX_DEV)
        factor = jnp.linalg.cholesky(kernel + shift_value * jnp.eye(docs_all, dtype=jnp.float32))
        first = lax.linalg.triangular_solve(factor, kernel, left_side=True, lower=True)
        second = lax.linalg.triangular_solve(factor, first, left_side=True, lower=True, transpose_a=True)
        score_list[section_id] = jnp.diagonal(second)
        adjoint_list[section_id] = new_adjoint
        adjoint_now = new_adjoint
    return (jnp.stack(adjoint_list), jnp.stack(score_list))
```

```python
import jax
import jax.numpy as jnp
from jax import lax
from jax.sharding import PartitionSpec as P

F32 = jnp.float32
BF16 = jnp.bfloat16
STEP = ((0, 1), (1, 0), (2, 3), (3, 2))
MIDDLE = ((1, 2), (2, 1))
TWO = ((0, 2), (2, 0), (1, 3), (3, 1))
ENDS = ((1, 0), (2, 3))
ACROSS = ((0, 3), (3, 0), (1, 2), (2, 1))
PAIR = ((0, 1), (1, 0))


def dot_t(a, b, **kw):
    return lax.dot_general(a, b, (((1,), (1,)), ((), ())), preferred_element_type=F32, **kw)


def after(x, *first):
    return lax.optimization_barrier((x, *first))[0]


def shifted(shard, axis, by):
    devices = lax.axis_size(axis)
    pairs = [(i, i + by) for i in range(devices) if 0 <= i + by < devices]
    return lax.ppermute(shard, axis, pairs)


def member_of(lengths, tok_rows):
    examples = lengths.shape[0]
    upto = jnp.arange(examples)[:, None] <= jnp.arange(examples)[None, :]
    ends = jnp.sum(jnp.where(upto, lengths[:, None], 0), axis=0)
    positions = jnp.arange(tok_rows, dtype=jnp.int32)
    doc_index = jnp.sum((positions[:, None] >= ends[None, :]).astype(jnp.int32), axis=1)
    return (doc_index[:, None] == jnp.arange(examples, dtype=jnp.int32)[None, :]).astype(F32)


def own_rows(out_proj, in_proj, lengths):
    member = member_of(lengths, out_proj.shape[0])
    rows = jnp.einsum("te,to,ti->eoi", member, out_proj, in_proj, precision=lax.Precision.HIGHEST)
    return rows.reshape(lengths.shape[0], -1).astype(BF16)


def scores_of(every_row, damping, start, examples, tok_rows):
    columns = every_row.shape[1]
    kernel = dot_t(every_row, every_row)
    shift_value = damping * (columns * tok_rows / examples)
    factor = jnp.linalg.cholesky(kernel + shift_value * jnp.eye(kernel.shape[0], dtype=F32))
    own_columns = lax.dynamic_slice_in_dim(kernel, start, examples, 1)
    first = lax.linalg.triangular_solve(factor, own_columns, left_side=True, lower=True)
    second = lax.linalg.triangular_solve(factor, first, left_side=True, lower=True, transpose_a=True)
    own_block = lax.dynamic_slice_in_dim(second, start, examples, 0)
    return jnp.sum(own_block * jnp.eye(examples, dtype=F32), axis=1)


def relay(acts, cotangent, in_weight, out_weight, in_factor, out_factor, damping, lengths):
    sections = lax.axis_size("section")
    section_index = lax.axis_index("section")
    tok_rows = cotangent.shape[0]
    examples = lengths.shape[1]
    u_full = lax.all_gather(in_weight[0], "dp", axis=0, tiled=True)
    v_full = lax.all_gather(out_weight[0], "dp", axis=0, tiled=True)
    adjoint_now = cotangent
    kept_rank = jnp.zeros((tok_rows, v_full.shape[0]), BF16)
    kept_adjoint = jnp.zeros_like(cotangent)
    for turn in range(sections):
        partial_rank = dot_t(adjoint_now, v_full)
        own_half = lax.psum_scatter(partial_rank, "mp", scatter_dimension=1, tiled=True).astype(BF16)
        rank_grad = lax.all_gather(own_half, "mp", axis=1, tiled=True)
        new_adjoint = (
            adjoint_now.astype(F32) + jnp.dot(rank_grad, u_full, preferred_element_type=F32)
        ).astype(BF16)
        active = section_index == sections - 1 - turn
        kept_rank = jnp.where(active, rank_grad, kept_rank)
        kept_adjoint = jnp.where(active, new_adjoint, kept_adjoint)
        if turn + 1 < sections:
            adjoint_now = shifted(new_adjoint, "section", -1)
    out_proj = dot_t(kept_rank, out_factor[0])
    in_proj = lax.psum(dot_t(acts[0], in_factor[0]), "mp")
    rows = own_rows(out_proj, in_proj, lengths[0])
    every_row = lax.all_gather(rows, "dp", axis=0, tiled=True)
    start = lax.axis_index("dp") * examples
    scores = scores_of(every_row, damping[0], start, examples, tok_rows)
    return (kept_adjoint[None], scores[None])


def gathered(w, *first):
    z = lax.axis_index("dp")
    w = after(w, *first)
    two = lax.ppermute(w, "dp", TWO)
    one = lax.ppermute(w, "dp", STEP)
    ends = lax.ppermute(two, "dp", ENDS)
    middle = lax.ppermute(after(w, two), "dp", MIDDLE)
    far = jnp.where((z == 0) | (z == 3), ends, middle)
    return [w, one, two, far]


def plane(axis):
    return (axis, PAIR) if axis != "both" else (("group", "section"), ACROSS)


def summed(part):
    core = lax.axis_index("mp")
    half = part.shape[1] // 2
    keep = lax.dynamic_slice_in_dim(part, core * half, half, 1)
    send = lax.dynamic_slice_in_dim(part, (1 - core) * half, half, 1)
    own = (keep + lax.ppermute(send, "mp", PAIR)).astype(BF16)
    others = [lax.ppermute(own, *plane(a)) for a in ("both", "section", "group")]
    total = own.astype(F32)
    for other in others:
        total = total + other.astype(F32)
    total = total.astype(BF16)
    other = lax.ppermute(total, "mp", PAIR)
    return jnp.where(core == 0, jnp.concatenate([total, other], 1), jnp.concatenate([other, total], 1))


def spread(acts, cotangent, in_weight, out_weight, in_factor, out_factor, damping, lengths):
    x, y, z = lax.axis_index("section"), lax.axis_index("group"), lax.axis_index("dp")
    tok_rows, width = cotangent.shape
    examples = lengths.shape[1]
    slice_width = width // 4

    def piece(a, px, py):
        return lax.dynamic_slice_in_dim(a, (px * 2 + py) * slice_width, slice_width, 1)

    v_own, u_own = out_weight[0], in_weight[0]
    v_keep, u_keep = piece(v_own, x, y), piece(u_own, x, y)
    v_other = lax.ppermute(piece(v_own, 1 - x, y), "section", PAIR)
    u_other = lax.ppermute(piece(u_own, 1 - x, y), "section", PAIR)
    last = x == 1
    v1, v0 = jnp.where(last, v_keep, v_other), jnp.where(last, v_other, v_keep)
    u1, u0 = jnp.where(last, u_keep, u_other), jnp.where(last, u_other, u_keep)
    g_own = piece(cotangent, x, y)
    g_other = lax.ppermute(piece(cotangent, x, 1 - y), "group", PAIR)
    g = jnp.where(y == 0, jnp.concatenate([g_own, g_other], 0), jnp.concatenate([g_other, g_own], 0))

    v1s = gathered(v1)
    u1s = gathered(u1, v1s[2])
    v0s = gathered(v0, u1s[2])
    u0s = gathered(u0, v0s[2])

    def step(adjoint, vs, us):
        part = jnp.concatenate([dot_t(adjoint, v) for v in vs], 1)
        rank = summed(part)
        block = rank.shape[1] // 4
        total = adjoint.astype(F32)
        for k, u in enumerate(us):
            total = total + jnp.dot(rank[:, k * block : (k + 1) * block], u, preferred_element_type=F32)
        return rank, total.astype(BF16)

    rank1, adjoint1 = step(g, v1s, u1s)
    rank0, adjoint0 = step(adjoint1, v0s, u0s)

    def of_group(a, who):
        return lax.dynamic_slice_in_dim(a, who * tok_rows, tok_rows, 0)

    mine, theirs = jnp.where(last, adjoint1, adjoint0), jnp.where(last, adjoint0, adjoint1)
    here = of_group(mine, y)
    from_x = lax.ppermute(of_group(theirs, y), *plane("section"))
    from_xy = lax.ppermute(of_group(theirs, 1 - y), *plane("both"))
    from_y = lax.ppermute(of_group(mine, 1 - y), *plane("group"))
    adjoint = jnp.zeros_like(cotangent)
    for value, px, py in ((here, x, y), (from_y, x, 1 - y), (from_x, 1 - x, y), (from_xy, 1 - x, 1 - y)):
        adjoint = lax.dynamic_update_slice_in_dim(adjoint, value, (px * 2 + py) * slice_width, 1)

    rank = of_group(jnp.where(last, rank1, rank0), y)
    block = out_factor.shape[2] // 4
    factor = jnp.concatenate(
        [lax.dynamic_slice_in_dim(out_factor[0], jnp.bitwise_xor(z, k) * block, block, 1) for k in range(4)], 1
    )
    out_proj = dot_t(rank, factor)
    in_part = dot_t(acts[0], in_factor[0])
    in_proj = in_part + lax.ppermute(in_part, "mp", PAIR)
    rows = own_rows(out_proj, in_proj, lengths[0])
    every_row = jnp.concatenate([rows] + [lax.ppermute(rows, "dp", p) for p in (STEP, TWO, ACROSS)], 0)
    scores = scores_of(every_row, damping[0], 0, examples, tok_rows)
    return (adjoint[None], scores[None])


def solution(mesh):
    sizes = (mesh.shape["group"], mesh.shape["dp"], mesh.shape["section"], mesh.shape["mp"])
    return jax.shard_map(
        spread if sizes == (2, 4, 2, 2) else relay,
        mesh=mesh,
        in_specs=(
            P("section", ("group", "dp"), "mp"),
            P(("group", "dp"), "mp"),
            P("section", "dp", "mp"),
            P("section", "dp", "mp"),
            P("section", None, "mp"),
            P("section", None, None),
            P("section"),
            P(("group", "dp"), None),
        ),
        out_specs=(P("section", ("group", "dp"), "mp"), P("section", ("group", "dp"))),
        check_vma=False,
    )
```

```python
import jax
import jax.numpy as jnp
from jax import lax
from jax.experimental import pallas as pl
from jax.experimental.pallas import tpu as pltpu
from jax.sharding import PartitionSpec as P

F32 = jnp.float32
BF16 = jnp.bfloat16
UP = ((0, 1), (1, 2), (2, 3), (3, 0))
DOWN = ((1, 0), (2, 1), (3, 2), (0, 3))
OPPOSITE = ((0, 2), (2, 0), (1, 3), (3, 1))
ACROSS = ((0, 3), (3, 0), (1, 2), (2, 1))
PAIR = ((0, 1), (1, 0))


def dot_t(a, b, **kw):
    return lax.dot_general(a, b, (((1,), (1,)), ((), ())), preferred_element_type=F32, **kw)


def after(x, *first):
    return lax.optimization_barrier((x, *first))[0]


def after2(xs, *first):
    return lax.optimization_barrier((*xs, *first))[: len(xs)]


def shifted(shard, axis, by):
    devices = lax.axis_size(axis)
    pairs = [(i, i + by) for i in range(devices) if 0 <= i + by < devices]
    return lax.ppermute(shard, axis, pairs)


def member_of(lengths, tok_rows):
    examples = lengths.shape[0]
    upto = jnp.arange(examples)[:, None] <= jnp.arange(examples)[None, :]
    ends = jnp.sum(jnp.where(upto, lengths[:, None], 0), axis=0)
    positions = jnp.arange(tok_rows, dtype=jnp.int32)
    doc_index = jnp.sum((positions[:, None] >= ends[None, :]).astype(jnp.int32), axis=1)
    return (doc_index[:, None] == jnp.arange(examples, dtype=jnp.int32)[None, :]).astype(F32)


def own_rows(out_proj, in_proj, lengths):
    member = member_of(lengths, out_proj.shape[0])
    rows = jnp.einsum("te,to,ti->eoi", member, out_proj, in_proj, precision=lax.Precision.HIGHEST)
    return rows.reshape(lengths.shape[0], -1).astype(BF16)


def scores_of(every_row, damping, start, examples, tok_rows):
    columns = every_row.shape[1]
    kernel = dot_t(every_row, every_row)
    shift_value = damping * (columns * tok_rows / examples)
    factor = jnp.linalg.cholesky(kernel + shift_value * jnp.eye(kernel.shape[0], dtype=F32))
    own_columns = lax.dynamic_slice_in_dim(kernel, start, examples, 1)
    first = lax.linalg.triangular_solve(factor, own_columns, left_side=True, lower=True)
    second = lax.linalg.triangular_solve(factor, first, left_side=True, lower=True, transpose_a=True)
    own_block = lax.dynamic_slice_in_dim(second, start, examples, 0)
    return jnp.sum(own_block * jnp.eye(examples, dtype=F32), axis=1)


def relay(acts, cotangent, in_weight, out_weight, in_factor, out_factor, damping, lengths):
    sections = lax.axis_size("section")
    section_index = lax.axis_index("section")
    tok_rows = cotangent.shape[0]
    examples = lengths.shape[1]
    u_full = lax.all_gather(in_weight[0], "dp", axis=0, tiled=True)
    v_full = lax.all_gather(out_weight[0], "dp", axis=0, tiled=True)
    adjoint_now = cotangent
    kept_rank = jnp.zeros((tok_rows, v_full.shape[0]), BF16)
    kept_adjoint = jnp.zeros_like(cotangent)
    for turn in range(sections):
        partial_rank = dot_t(adjoint_now, v_full)
        own_half = lax.psum_scatter(partial_rank, "mp", scatter_dimension=1, tiled=True).astype(BF16)
        rank_grad = lax.all_gather(own_half, "mp", axis=1, tiled=True)
        new_adjoint = (
            adjoint_now.astype(F32) + jnp.dot(rank_grad, u_full, preferred_element_type=F32)
        ).astype(BF16)
        active = section_index == sections - 1 - turn
        kept_rank = jnp.where(active, rank_grad, kept_rank)
        kept_adjoint = jnp.where(active, new_adjoint, kept_adjoint)
        if turn + 1 < sections:
            adjoint_now = shifted(new_adjoint, "section", -1)
    out_proj = dot_t(kept_rank, out_factor[0])
    in_proj = lax.psum(dot_t(acts[0], in_factor[0]), "mp")
    rows = own_rows(out_proj, in_proj, lengths[0])
    every_row = lax.all_gather(rows, "dp", axis=0, tiled=True)
    start = lax.axis_index("dp") * examples
    scores = scores_of(every_row, damping[0], start, examples, tok_rows)
    return (kept_adjoint[None], scores[None])


def gathered(w, name):
    half = w.shape[0] // 2
    with jax.named_scope(name):
        below, above = lax.ppermute(w, "dp", UP), lax.ppermute(w, "dp", DOWN)
        upper, lower = lax.ppermute(below[:half], "dp", UP), lax.ppermute(above[half:], "dp", DOWN)
    return [w, below, above, upper, lower]


def plane(axis):
    return (axis, PAIR) if axis != "both" else (("group", "section"), ACROSS)


def summed(keep, send, gate1, gate2):
    own = after((keep + lax.ppermute(send, "mp", PAIR)).astype(BF16), *gate1)
    others = [lax.ppermute(own, *plane(a)) for a in ("both", "section", "group")]
    total = own.astype(F32)
    for other in others:
        total = total + other.astype(F32)
    total = after(total.astype(BF16), *gate2)
    return total, lax.ppermute(total, "mp", PAIR)


class Copies:
    def __init__(self, sems):
        self.sems, self.used, self.waits = sems, 0, []

    def start(self, pairs):
        for src, dst in pairs:
            copy = pltpu.make_async_copy(src, dst, self.sems.at[self.used])
            copy.start()
            self.waits.append(copy)
            self.used += 1

    def start_either(self, which, ifs, elses):
        first = self.used
        for holds, pairs in ((which, ifs), (jnp.logical_not(which), elses)):

            @pl.when(holds)
            def _():
                for k, (src, dst) in enumerate(pairs):
                    pltpu.make_async_copy(src, dst, self.sems.at[first + k]).start()

        for k, (src, dst) in enumerate(ifs):
            self.waits.append(pltpu.make_async_copy(src, dst, self.sems.at[first + k]))
        self.used += len(ifs)

    def wait(self):
        for copy in self.waits:
            copy.wait()
        self.waits = []


def rows_into(slot, dst, which=0):
    n, starts = dst.shape[0] // 8, []
    for ref in slot[:3]:
        starts += [(ref, which * n), (ref, ref.shape[0] // 2 + which * n)]
    starts += [(ref, which * n) for ref in slot[3:]]
    return [(ref.at[pl.ds(at, n)], dst.at[pl.ds(k * n, n)]) for k, (ref, at) in enumerate(starts)]


def halves_into(mine, other, dst, core):
    half = mine.shape[1]
    return [
        (mine, dst.at[:, pl.ds(pl.multiple_of(core * half, half), half)]),
        (other, dst.at[:, pl.ds(pl.multiple_of((1 - core) * half, half), half)]),
    ]


def groups_into(own, other, dst, y):
    n = own.shape[0]
    return [
        (own, dst.at[pl.ds(pl.multiple_of(y * n, n), n)]),
        (other, dst.at[pl.ds(pl.multiple_of((1 - y) * n, n), n)]),
    ]


def write_part(adjoint, vs, keep, send, part, core):
    half = keep.shape[1]
    for k in range(2):
        part[k] = dot_t(adjoint[...], vs[k * half : (k + 1) * half, :])
    keep[...] = part[core]
    send[...] = part[1 - core]


def add_ranked(adjoint, rank, us, out, step):
    for at in range(0, adjoint.shape[1], step):
        columns = slice(at, at + step)
        delta = jnp.dot(rank[...], us[:, columns], preferred_element_type=F32)
        out[:, columns] = (adjoint[:, columns].astype(F32) + delta).astype(BF16)


def first_kernel(flags, g_own, g_other, *refs):
    slot1, slot2, (keep, send, g, vs, part, sems) = refs[:5], refs[5:10], refs[10:]
    last, y, core = flags[0] == 1, flags[1], flags[2]
    copies = Copies(sems)
    copies.start(groups_into(g_own, g_other, g, y))
    copies.start_either(last, rows_into(slot1, vs), rows_into(slot2, vs))
    copies.wait()
    write_part(g, vs, keep, send, part, core)


def middle_kernel(flags, g_own, g_other, mine, other, *refs):
    slot1, slot2, rest = refs[:5], refs[5:10], refs[10:15]
    adjoint, keep, send, g, rank, us, vs, part, sems = refs[15:]
    last, y, core = flags[0] == 1, flags[1], flags[2]
    copies = Copies(sems)
    copies.start(groups_into(g_own, g_other, g, y) + halves_into(mine, other, rank, core))
    copies.start_either(last, rows_into(slot2, us), rows_into(rest, us))
    copies.start_either(last, rows_into(rest, vs), rows_into(slot1, vs))
    copies.wait()
    add_ranked(g, rank, us, adjoint, 256)
    write_part(adjoint, vs, keep, send, part, core)


def last_kernel(flags, adjoint1, mine, other, *refs):
    rest, (here, to_x, to_xy, to_y, kept, rank, us, adjoint0, sems) = refs[:5], refs[5:]
    last, y, core = flags[0] == 1, flags[1], flags[2]
    n = here.shape[0]
    copies = Copies(sems)
    copies.start([(adjoint1, kept)] + halves_into(mine, other, rank, core))
    copies.start(rows_into(rest, us, 1))
    copies.wait()
    add_ranked(kept, rank, us, adjoint0, 256)

    def sends(own, others):
        return [
            (others.at[pl.ds(pl.multiple_of(y * n, n), n)], to_x),
            (others.at[pl.ds(pl.multiple_of((1 - y) * n, n), n)], to_xy),
            (own.at[pl.ds(pl.multiple_of((1 - y) * n, n), n)], to_y),
            (own.at[pl.ds(pl.multiple_of(y * n, n), n)], here),
        ]

    copies.start_either(last, sends(kept, adjoint0), sends(adjoint0, kept))
    copies.wait()


def kernel_call(body, name, outs, scratch, copies, flags, *args):
    anywhere = pl.BlockSpec(memory_space=pltpu.HBM)
    return pl.pallas_call(
        body,
        name=name,
        out_shape=[o for o, _ in outs],
        in_specs=[pl.BlockSpec(memory_space=pltpu.SMEM)] + [anywhere] * len(args),
        out_specs=[anywhere if far else pl.BlockSpec(memory_space=pltpu.VMEM) for _, far in outs],
        scratch_shapes=[pltpu.VMEM(*shape) for shape in scratch] + [pltpu.SemaphoreType.DMA((copies,))],
        compiler_params=pltpu.CompilerParams(vmem_limit_bytes=16 << 20),
    )(flags, *[pltpu.with_memory_space_constraint(a, pltpu.HBM) for a in args])


def spread(acts, cotangent, in_weight, out_weight, in_factor, out_factor, damping, lengths):
    x, y, z = lax.axis_index("section"), lax.axis_index("group"), lax.axis_index("dp")
    tok_rows, width = cotangent.shape
    examples = lengths.shape[1]
    slice_width = width // 4

    def piece(a, px, py):
        return lax.dynamic_slice_in_dim(a, (px * 2 + py) * slice_width, slice_width, 1)

    v_own, u_own = out_weight[0], in_weight[0]
    last = x == 1

    n = v_own.shape[0]
    v_keep, u_keep = piece(v_own, x, y), piece(u_own, x, y)
    slot1 = gathered(v_keep, "slot1")
    v_other = lax.ppermute(piece(v_own, 1 - x, y), "section", PAIR)
    u_other = lax.ppermute(piece(u_own, 1 - x, y), "section", PAIR)
    g_own = piece(cotangent, x, y)
    g_other = lax.ppermute(piece(cotangent, x, 1 - y), "group", PAIR)
    slot2 = gathered(jnp.where(last, u_keep, v_other), "slot2")
    u_keep, v_other, u_other = after2((u_keep, v_other, u_other), slot1[1])
    h = n // 2
    third, fourth = jnp.where(last, v_other, u_other), jnp.where(last, u_other, u_keep)
    rest = gathered(jnp.concatenate([third[:h], fourth[:h], third[h:], fourth[h:]], 0), "slot34")

    flags = jnp.stack([x, y, lax.axis_index("mp")]).astype(jnp.int32)
    groups = lax.axis_size("group")
    ranks = 4 * n
    tokens = groups * tok_rows
    half_part = jax.ShapeDtypeStruct((tokens, ranks // 2), F32)
    shape_of = jax.ShapeDtypeStruct((tokens, slice_width), BF16)
    send_of = jax.ShapeDtypeStruct((tok_rows, slice_width), BF16)
    wide, rank_of = ((tokens, slice_width), BF16), ((tokens, ranks), BF16)
    weight, part_of = ((ranks, slice_width), BF16), ((2, tokens, ranks // 2), F32)

    keep, send = kernel_call(
        first_kernel, "first", [(half_part, False)] * 2, [wide, weight, part_of], 10, flags, g_own, g_other, *slot1, *slot2
    )
    mine1, other1 = summed(keep, send, rest[1:2], rest[3:])
    adjoint1, keep, send = kernel_call(
        middle_kernel, "middle", [(shape_of, False), (half_part, False), (half_part, False)],
        [wide, rank_of, weight, weight, part_of], 20, flags, g_own, g_other, mine1, other1, *slot1, *slot2, *rest,
    )
    mine0, other0 = summed(keep, send, (), ())
    here, to_x, to_xy, to_y = kernel_call(
        last_kernel, "last", [(send_of, True)] * 4, [wide, rank_of, weight, wide], 15, flags, adjoint1, mine0, other0, *rest
    )
    from_xy = lax.ppermute(to_xy, *plane("both"))
    from_x = lax.ppermute(to_x, *plane("section"))
    from_y = lax.ppermute(to_y, *plane("group"))

    def of_group(a, who):
        return lax.dynamic_slice_in_dim(a, who * tok_rows, tok_rows, 0)

    adjoint = jnp.zeros_like(cotangent)
    for value, px, py in ((here, x, y), (from_y, x, 1 - y), (from_x, 1 - x, y), (from_xy, 1 - x, 1 - y)):
        adjoint = lax.dynamic_update_slice_in_dim(adjoint, value, (px * 2 + py) * slice_width, 1)

    core = lax.axis_index("mp")
    mine, other = of_group(jnp.where(last, mine1, mine0), y), of_group(jnp.where(last, other1, other0), y)
    rank = jnp.where(core == 0, jnp.concatenate([mine, other], 1), jnp.concatenate([other, mine], 1))
    block = out_factor.shape[2] // 4
    factor = jnp.concatenate(
        [lax.dynamic_slice_in_dim(out_factor[0], lax.rem(z + k, 4) * block, block, 1) for k in (0, 3, 1, 2)], 1
    )
    out_proj = dot_t(rank, factor)
    in_part = dot_t(acts[0], in_factor[0])
    in_proj = in_part + lax.ppermute(in_part, "mp", PAIR)
    rows = own_rows(out_proj, in_proj, lengths[0])
    every_row = jnp.concatenate([rows] + [lax.ppermute(rows, "dp", p) for p in (UP, DOWN, OPPOSITE)], 0)
    every_row = after(every_row, from_x, from_y)
    scores = scores_of(every_row, damping[0], 0, examples, tok_rows)
    return (adjoint[None], scores[None])


def solution(mesh):
    sizes = (mesh.shape["group"], mesh.shape["dp"], mesh.shape["section"], mesh.shape["mp"])
    return jax.shard_map(
        spread if sizes == (2, 4, 2, 2) else relay,
        mesh=mesh,
        in_specs=(
            P("section", ("group", "dp"), "mp"),
            P(("group", "dp"), "mp"),
            P("section", "dp", "mp"),
            P("section", "dp", "mp"),
            P("section", None, "mp"),
            P("section", None, None),
            P("section"),
            P(("group", "dp"), None),
        ),
        out_specs=(P("section", ("group", "dp"), "mp"), P("section", ("group", "dp"))),
        check_vma=False,
    )
```

```python
import jax
import jax.numpy as jnp
from jax import lax
from jax.experimental import pallas as pl
from jax.experimental.pallas import tpu as pltpu
from jax.sharding import PartitionSpec as P

F32 = jnp.float32
BF16 = jnp.bfloat16
UP = ((0, 1), (1, 2), (2, 3), (3, 0))
DOWN = ((1, 0), (2, 1), (3, 2), (0, 3))
OPPOSITE = ((0, 2), (2, 0), (1, 3), (3, 1))
ACROSS = ((0, 3), (3, 0), (1, 2), (2, 1))
PAIR = ((0, 1), (1, 0))


def dot_t(a, b, **kw):
    return lax.dot_general(a, b, (((1,), (1,)), ((), ())), preferred_element_type=F32, **kw)


def after(x, *first):
    return lax.optimization_barrier((x, *first))[0]


def after2(xs, *first):
    return lax.optimization_barrier((*xs, *first))[: len(xs)]


def shifted(shard, axis, by):
    devices = lax.axis_size(axis)
    pairs = [(i, i + by) for i in range(devices) if 0 <= i + by < devices]
    return lax.ppermute(shard, axis, pairs)


def member_of(lengths, tok_rows):
    examples = lengths.shape[0]
    upto = jnp.arange(examples)[:, None] <= jnp.arange(examples)[None, :]
    ends = jnp.sum(jnp.where(upto, lengths[:, None], 0), axis=0)
    positions = jnp.arange(tok_rows, dtype=jnp.int32)
    doc_index = jnp.sum((positions[:, None] >= ends[None, :]).astype(jnp.int32), axis=1)
    return (doc_index[:, None] == jnp.arange(examples, dtype=jnp.int32)[None, :]).astype(F32)


def own_rows(out_proj, in_proj, lengths):
    member = member_of(lengths, out_proj.shape[0])
    rows = jnp.einsum("te,to,ti->eoi", member, out_proj, in_proj, precision=lax.Precision.HIGHEST)
    return rows.reshape(lengths.shape[0], -1).astype(BF16)


def scores_of(every_row, damping, start, examples, tok_rows):
    columns = every_row.shape[1]
    kernel = dot_t(every_row, every_row)
    shift_value = damping * (columns * tok_rows / examples)
    factor = jnp.linalg.cholesky(kernel + shift_value * jnp.eye(kernel.shape[0], dtype=F32))
    own_columns = lax.dynamic_slice_in_dim(kernel, start, examples, 1)
    first = lax.linalg.triangular_solve(factor, own_columns, left_side=True, lower=True)
    second = lax.linalg.triangular_solve(factor, first, left_side=True, lower=True, transpose_a=True)
    own_block = lax.dynamic_slice_in_dim(second, start, examples, 0)
    return jnp.sum(own_block * jnp.eye(examples, dtype=F32), axis=1)


def relay(acts, cotangent, in_weight, out_weight, in_factor, out_factor, damping, lengths):
    sections = lax.axis_size("section")
    section_index = lax.axis_index("section")
    tok_rows = cotangent.shape[0]
    examples = lengths.shape[1]
    u_full = lax.all_gather(in_weight[0], "dp", axis=0, tiled=True)
    v_full = lax.all_gather(out_weight[0], "dp", axis=0, tiled=True)
    adjoint_now = cotangent
    kept_rank = jnp.zeros((tok_rows, v_full.shape[0]), BF16)
    kept_adjoint = jnp.zeros_like(cotangent)
    for turn in range(sections):
        partial_rank = dot_t(adjoint_now, v_full)
        own_half = lax.psum_scatter(partial_rank, "mp", scatter_dimension=1, tiled=True).astype(BF16)
        rank_grad = lax.all_gather(own_half, "mp", axis=1, tiled=True)
        new_adjoint = (
            adjoint_now.astype(F32) + jnp.dot(rank_grad, u_full, preferred_element_type=F32)
        ).astype(BF16)
        active = section_index == sections - 1 - turn
        kept_rank = jnp.where(active, rank_grad, kept_rank)
        kept_adjoint = jnp.where(active, new_adjoint, kept_adjoint)
        if turn + 1 < sections:
            adjoint_now = shifted(new_adjoint, "section", -1)
    out_proj = dot_t(kept_rank, out_factor[0])
    in_proj = lax.psum(dot_t(acts[0], in_factor[0]), "mp")
    rows = own_rows(out_proj, in_proj, lengths[0])
    every_row = lax.all_gather(rows, "dp", axis=0, tiled=True)
    start = lax.axis_index("dp") * examples
    scores = scores_of(every_row, damping[0], start, examples, tok_rows)
    return (kept_adjoint[None], scores[None])


def gathered(w, name):
    half = w.shape[0] // 2
    with jax.named_scope(name):
        below, above = lax.ppermute(w, "dp", UP), lax.ppermute(w, "dp", DOWN)
        upper, lower = lax.ppermute(below[:half], "dp", UP), lax.ppermute(above[half:], "dp", DOWN)
    return [w, below, above, upper, lower]


def plane(axis):
    return (axis, PAIR) if axis != "both" else (("group", "section"), ACROSS)


def summed(keep, send, gate1, gate2):
    own = after((keep + lax.ppermute(send, "mp", PAIR)).astype(BF16), *gate1)
    others = [lax.ppermute(own, *plane(a)) for a in ("both", "section", "group")]
    total = own.astype(F32)
    for other in others:
        total = total + other.astype(F32)
    total = after(total.astype(BF16), *gate2)
    return total, lax.ppermute(total, "mp", PAIR)


class Copies:
    def __init__(self, sems):
        self.sems, self.used, self.waits = sems, 0, []

    def start(self, pairs):
        for src, dst in pairs:
            copy = pltpu.make_async_copy(src, dst, self.sems.at[self.used])
            copy.start()
            self.waits.append(copy)
            self.used += 1

    def start_either(self, which, ifs, elses):
        first = self.used
        for holds, pairs in ((which, ifs), (jnp.logical_not(which), elses)):

            @pl.when(holds)
            def _():
                for k, (src, dst) in enumerate(pairs):
                    pltpu.make_async_copy(src, dst, self.sems.at[first + k]).start()

        for k, (src, dst) in enumerate(ifs):
            self.waits.append(pltpu.make_async_copy(src, dst, self.sems.at[first + k]))
        self.used += len(ifs)

    def wait(self):
        for copy in self.waits:
            copy.wait()
        self.waits = []


def rows_into(slot, dst, which=0):
    n, starts = dst.shape[0] // 8, []
    for ref in slot[:3]:
        starts += [(ref, which * n), (ref, ref.shape[0] // 2 + which * n)]
    starts += [(ref, 0) for ref in slot[3:]]
    return [(ref.at[pl.ds(at, n)], dst.at[pl.ds(k * n, n)]) for k, (ref, at) in enumerate(starts)]


def halves_into(mine, other, dst, core):
    half = mine.shape[1]
    return [
        (mine, dst.at[:, pl.ds(pl.multiple_of(core * half, half), half)]),
        (other, dst.at[:, pl.ds(pl.multiple_of((1 - core) * half, half), half)]),
    ]


def groups_into(own, other, dst, y):
    n = own.shape[0]
    return [
        (own, dst.at[pl.ds(pl.multiple_of(y * n, n), n)]),
        (other, dst.at[pl.ds(pl.multiple_of((1 - y) * n, n), n)]),
    ]


def write_part(adjoint, vs, keep, send, part, core):
    half = keep.shape[1]
    for k in range(2):
        part[k] = dot_t(adjoint[...], vs[k * half : (k + 1) * half, :])
    keep[...] = part[core]
    send[...] = part[1 - core]


def add_ranked(adjoint, rank, us, out, step):
    for at in range(0, adjoint.shape[1], step):
        columns = slice(at, at + step)
        delta = jnp.dot(rank[...], us[:, columns], preferred_element_type=F32)
        out[:, columns] = (adjoint[:, columns].astype(F32) + delta).astype(BF16)


def first_kernel(flags, g_own, g_other, *refs):
    slot1, slot2, (keep, send, g, vs, part, sems) = refs[:5], refs[5:10], refs[10:]
    last, y, core = flags[0] == 1, flags[1], flags[2]
    copies = Copies(sems)
    copies.start(groups_into(g_own, g_other, g, y))
    copies.start_either(last, rows_into(slot1, vs), rows_into(slot2, vs))
    copies.wait()
    write_part(g, vs, keep, send, part, core)


def middle_kernel(flags, g_own, g_other, mine, other, *refs):
    slot1, slot2, rest = refs[:5], refs[5:10], refs[10:15]
    adjoint, keep, send, g, rank, us, vs, part, sems = refs[15:]
    last, y, core = flags[0] == 1, flags[1], flags[2]
    copies = Copies(sems)
    copies.start(groups_into(g_own, g_other, g, y) + halves_into(mine, other, rank, core))
    copies.start_either(last, rows_into(slot2, us), rows_into(rest, us))
    copies.start_either(last, rows_into(rest, vs), rows_into(slot1, vs))
    copies.wait()
    add_ranked(g, rank, us, adjoint, 256)
    write_part(adjoint, vs, keep, send, part, core)


def last_kernel(flags, adjoint1, mine, other, *refs):
    rest, (here, to_x, to_xy, to_y, kept, rank, us, adjoint0, sems) = refs[:5], refs[5:]
    last, y, core = flags[0] == 1, flags[1], flags[2]
    n = here.shape[0]
    copies = Copies(sems)
    copies.start([(adjoint1, kept)] + halves_into(mine, other, rank, core))
    copies.start(rows_into(rest, us, 1))
    copies.wait()
    add_ranked(kept, rank, us, adjoint0, 256)

    def sends(own, others):
        return [
            (others.at[pl.ds(pl.multiple_of(y * n, n), n)], to_x),
            (others.at[pl.ds(pl.multiple_of((1 - y) * n, n), n)], to_xy),
            (own.at[pl.ds(pl.multiple_of((1 - y) * n, n), n)], to_y),
            (own.at[pl.ds(pl.multiple_of(y * n, n), n)], here),
        ]

    copies.start_either(last, sends(kept, adjoint0), sends(adjoint0, kept))
    copies.wait()


def score_kernel(shift, *refs):
    rows, (out, stacked) = refs[:-2], refs[-2:]
    n = rows[0].shape[0]
    for k, ref in enumerate(rows):
        stacked[k * n : (k + 1) * n, :] = ref[...].astype(F32)
    every = stacked[...].astype(BF16)
    kernel = dot_t(every, every)
    order = kernel.shape[0]
    row = lax.broadcasted_iota(jnp.int32, (order, order), 0)
    column = lax.broadcasted_iota(jnp.int32, (order, order), 1)
    left = kernel + jnp.where(row == column, shift[0], 0.0)
    right = kernel
    for k in range(order):
        inverse = 1.0 / left[k : k + 1, k : k + 1]
        left_row, right_row = left[k : k + 1, :] * inverse, right[k : k + 1, :] * inverse
        factor = left[:, k : k + 1]
        left = jnp.where(row == k, left_row, left - factor * left_row)
        right = jnp.where(row == k, right_row, right - factor * right_row)
    out[...] = jnp.sum(jnp.where(row == column, right, 0.0), axis=0, keepdims=True)


def scores_by_kernel(blocks, shift):
    order = len(blocks) * blocks[0].shape[0]
    return pl.pallas_call(
        score_kernel,
        name="scores",
        out_shape=jax.ShapeDtypeStruct((1, order), F32),
        in_specs=[pl.BlockSpec(memory_space=pltpu.SMEM)] + [pl.BlockSpec(memory_space=pltpu.VMEM)] * len(blocks),
        out_specs=pl.BlockSpec(memory_space=pltpu.VMEM),
        scratch_shapes=[pltpu.VMEM((order, blocks[0].shape[1]), F32)],
        compiler_params=pltpu.CompilerParams(vmem_limit_bytes=8 << 20),
    )(shift, *blocks)


def kernel_call(body, name, outs, scratch, copies, flags, *args):
    anywhere = pl.BlockSpec(memory_space=pl.ANY)
    return pl.pallas_call(
        body,
        name=name,
        out_shape=[o for o, _ in outs],
        in_specs=[pl.BlockSpec(memory_space=pltpu.SMEM)] + [anywhere] * len(args),
        out_specs=[anywhere if far else pl.BlockSpec(memory_space=pltpu.VMEM) for _, far in outs],
        scratch_shapes=[pltpu.VMEM(*shape) for shape in scratch] + [pltpu.SemaphoreType.DMA((copies,))],
        compiler_params=pltpu.CompilerParams(vmem_limit_bytes=16 << 20),
    )(flags, *[pltpu.with_memory_space_constraint(a, pltpu.HBM) if a.shape[1] > 512 else a for a in args])


def spread(acts, cotangent, in_weight, out_weight, in_factor, out_factor, damping, lengths):
    x, y, z = lax.axis_index("section"), lax.axis_index("group"), lax.axis_index("dp")
    tok_rows, width = cotangent.shape
    examples = lengths.shape[1]
    slice_width = width // 4

    def piece(a, px, py):
        return lax.dynamic_slice_in_dim(a, (px * 2 + py) * slice_width, slice_width, 1)

    v_own, u_own = out_weight[0], in_weight[0]
    last = x == 1

    n = v_own.shape[0]
    v_keep, u_keep = piece(v_own, x, y), piece(u_own, x, y)
    slot1 = gathered(v_keep, "slot1")
    v_other = lax.ppermute(piece(v_own, 1 - x, y), "section", PAIR)
    u_other = lax.ppermute(piece(u_own, 1 - x, y), "section", PAIR)
    g_own = piece(cotangent, x, y)
    g_other = lax.ppermute(piece(cotangent, x, 1 - y), "group", PAIR)
    slot2 = gathered(jnp.where(last, u_keep, v_other), "slot2")
    u_keep, v_other, u_other = after2((u_keep, v_other, u_other), *slot2[1:3])
    h = n // 2
    third, fourth = jnp.where(last, v_other, u_other), jnp.where(last, u_other, u_keep)
    both = jnp.concatenate([third[:h], fourth[:h], third[h:], fourth[h:]], 0)
    with jax.named_scope("slot34"):
        below, above = lax.ppermute(both, "dp", UP), lax.ppermute(both, "dp", DOWN)
    with jax.named_scope("slot3"):
        far3 = [lax.ppermute(below[:h], "dp", UP), lax.ppermute(above[n : n + h], "dp", DOWN)]
    with jax.named_scope("slot4"):
        ready = after2((below[h:n], above[n + h :]), *far3[:1])
        far4 = [lax.ppermute(ready[0], "dp", UP), lax.ppermute(ready[1], "dp", DOWN)]
    slot3, slot4 = [both, below, above, *far3], [both, below, above, *far4]

    flags = jnp.stack([x, y, lax.axis_index("mp")]).astype(jnp.int32)
    groups = lax.axis_size("group")
    ranks = 4 * n
    tokens = groups * tok_rows
    half_part = jax.ShapeDtypeStruct((tokens, ranks // 2), F32)
    shape_of = jax.ShapeDtypeStruct((tokens, slice_width), BF16)
    send_of = jax.ShapeDtypeStruct((tok_rows, slice_width), BF16)
    wide, rank_of = ((tokens, slice_width), BF16), ((tokens, ranks), BF16)
    weight, part_of = ((ranks, slice_width), BF16), ((2, tokens, ranks // 2), F32)

    keep, send = kernel_call(
        first_kernel, "first", [(half_part, False)] * 2, [wide, weight, part_of], 10, flags, g_own, g_other, *slot1, *slot2
    )
    mine1, other1 = summed(keep, send, slot3[1:2], slot3[3:])
    adjoint1, keep, send = kernel_call(
        middle_kernel, "middle", [(shape_of, False), (half_part, False), (half_part, False)],
        [wide, rank_of, weight, weight, part_of], 20, flags, g_own, g_other, mine1, other1, *slot1, *slot2, *slot3,
    )
    mine0, other0 = summed(keep, send, (), slot4[3:])
    here, to_x, to_xy, to_y = kernel_call(
        last_kernel, "last", [(send_of, True)] * 4, [wide, rank_of, weight, wide], 15, flags, adjoint1, mine0, other0, *slot4
    )
    from_xy = lax.ppermute(to_xy, *plane("both"))
    from_x = lax.ppermute(to_x, *plane("section"))
    from_y = lax.ppermute(to_y, *plane("group"))

    def of_group(a, who):
        return lax.dynamic_slice_in_dim(a, who * tok_rows, tok_rows, 0)

    adjoint = jnp.zeros_like(cotangent)
    for value, px, py in ((here, x, y), (from_y, x, 1 - y), (from_x, 1 - x, y), (from_xy, 1 - x, 1 - y)):
        adjoint = lax.dynamic_update_slice_in_dim(adjoint, value, (px * 2 + py) * slice_width, 1)

    core = lax.axis_index("mp")
    mine, other = of_group(jnp.where(last, mine1, mine0), y), of_group(jnp.where(last, other1, other0), y)
    rank = jnp.where(core == 0, jnp.concatenate([mine, other], 1), jnp.concatenate([other, mine], 1))
    block = out_factor.shape[2] // 4
    factor = jnp.concatenate(
        [lax.dynamic_slice_in_dim(out_factor[0], lax.rem(z + k, 4) * block, block, 1) for k in (0, 3, 1, 2)], 1
    )
    out_proj = dot_t(rank, factor)
    in_part = dot_t(acts[0], in_factor[0])
    in_proj = in_part + lax.ppermute(in_part, "mp", PAIR)
    rows = own_rows(out_proj, in_proj, lengths[0])
    rows = after(rows, from_x)
    blocks = [rows] + [lax.ppermute(rows, "dp", p) for p in (UP, DOWN, OPPOSITE)]
    columns = rows.shape[1]
    scores = scores_by_kernel(blocks, damping * (columns * tok_rows / examples))[:, :examples]
    return (adjoint[None], scores)


def solution(mesh):
    sizes = (mesh.shape["group"], mesh.shape["dp"], mesh.shape["section"], mesh.shape["mp"])
    return jax.shard_map(
        spread if sizes == (2, 4, 2, 2) else relay,
        mesh=mesh,
        in_specs=(
            P("section", ("group", "dp"), "mp"),
            P(("group", "dp"), "mp"),
            P("section", "dp", "mp"),
            P("section", "dp", "mp"),
            P("section", None, "mp"),
            P("section", None, None),
            P("section"),
            P(("group", "dp"), None),
        ),
        out_specs=(P("section", ("group", "dp"), "mp"), P("section", ("group", "dp"))),
        check_vma=False,
    )
```

```python
import jax
import jax.numpy as jnp
from jax import lax
from jax.experimental import pallas as pl
from jax.experimental.pallas import tpu as pltpu
from jax.sharding import PartitionSpec as P

F32 = jnp.float32
BF16 = jnp.bfloat16
UP = ((0, 1), (1, 2), (2, 3), (3, 0))
DOWN = ((1, 0), (2, 1), (3, 2), (0, 3))
OPPOSITE = ((0, 2), (2, 0), (1, 3), (3, 1))
ACROSS = ((0, 3), (3, 0), (1, 2), (2, 1))
PAIR = ((0, 1), (1, 0))


def dot_t(a, b, **kw):
    return lax.dot_general(a, b, (((1,), (1,)), ((), ())), preferred_element_type=F32, **kw)


def after(x, *first):
    return lax.optimization_barrier((x, *first))[0]


def after2(xs, *first):
    return lax.optimization_barrier((*xs, *first))[: len(xs)]


def shifted(shard, axis, by):
    devices = lax.axis_size(axis)
    pairs = [(i, i + by) for i in range(devices) if 0 <= i + by < devices]
    return lax.ppermute(shard, axis, pairs)


def member_of(lengths, tok_rows):
    examples = lengths.shape[0]
    upto = jnp.arange(examples)[:, None] <= jnp.arange(examples)[None, :]
    ends = jnp.sum(jnp.where(upto, lengths[:, None], 0), axis=0)
    positions = jnp.arange(tok_rows, dtype=jnp.int32)
    doc_index = jnp.sum((positions[:, None] >= ends[None, :]).astype(jnp.int32), axis=1)
    return (doc_index[:, None] == jnp.arange(examples, dtype=jnp.int32)[None, :]).astype(F32)


def own_rows(out_proj, in_proj, lengths):
    member = member_of(lengths, out_proj.shape[0])
    rows = jnp.einsum("te,to,ti->eoi", member, out_proj, in_proj, precision=lax.Precision.HIGHEST)
    return rows.reshape(lengths.shape[0], -1).astype(BF16)


def scores_of(every_row, damping, start, examples, tok_rows):
    columns = every_row.shape[1]
    kernel = dot_t(every_row, every_row)
    shift_value = damping * (columns * tok_rows / examples)
    factor = jnp.linalg.cholesky(kernel + shift_value * jnp.eye(kernel.shape[0], dtype=F32))
    own_columns = lax.dynamic_slice_in_dim(kernel, start, examples, 1)
    first = lax.linalg.triangular_solve(factor, own_columns, left_side=True, lower=True)
    second = lax.linalg.triangular_solve(factor, first, left_side=True, lower=True, transpose_a=True)
    own_block = lax.dynamic_slice_in_dim(second, start, examples, 0)
    return jnp.sum(own_block * jnp.eye(examples, dtype=F32), axis=1)


def relay(acts, cotangent, in_weight, out_weight, in_factor, out_factor, damping, lengths):
    sections = lax.axis_size("section")
    section_index = lax.axis_index("section")
    tok_rows = cotangent.shape[0]
    examples = lengths.shape[1]
    u_full = lax.all_gather(in_weight[0], "dp", axis=0, tiled=True)
    v_full = lax.all_gather(out_weight[0], "dp", axis=0, tiled=True)
    adjoint_now = cotangent
    kept_rank = jnp.zeros((tok_rows, v_full.shape[0]), BF16)
    kept_adjoint = jnp.zeros_like(cotangent)
    for turn in range(sections):
        partial_rank = dot_t(adjoint_now, v_full)
        own_half = lax.psum_scatter(partial_rank, "mp", scatter_dimension=1, tiled=True).astype(BF16)
        rank_grad = lax.all_gather(own_half, "mp", axis=1, tiled=True)
        new_adjoint = (
            adjoint_now.astype(F32) + jnp.dot(rank_grad, u_full, preferred_element_type=F32)
        ).astype(BF16)
        active = section_index == sections - 1 - turn
        kept_rank = jnp.where(active, rank_grad, kept_rank)
        kept_adjoint = jnp.where(active, new_adjoint, kept_adjoint)
        if turn + 1 < sections:
            adjoint_now = shifted(new_adjoint, "section", -1)
    out_proj = dot_t(kept_rank, out_factor[0])
    in_proj = lax.psum(dot_t(acts[0], in_factor[0]), "mp")
    rows = own_rows(out_proj, in_proj, lengths[0])
    every_row = lax.all_gather(rows, "dp", axis=0, tiled=True)
    start = lax.axis_index("dp") * examples
    scores = scores_of(every_row, damping[0], start, examples, tok_rows)
    return (kept_adjoint[None], scores[None])


def gathered(w, name):
    half = w.shape[0] // 2
    with jax.named_scope(name):
        below, above = lax.ppermute(w, "dp", UP), lax.ppermute(w, "dp", DOWN)
        upper, lower = lax.ppermute(below[:half], "dp", UP), lax.ppermute(above[half:], "dp", DOWN)
    return [w, below, above, upper, lower]


def plane(axis):
    return (axis, PAIR) if axis != "both" else (("group", "section"), ACROSS)


def summed(keep, send, sent_as, gate1, gate2):
    own = after((keep + lax.ppermute(send, "mp", PAIR)).astype(sent_as), *gate1)
    others = [lax.ppermute(own, *plane(a)) for a in ("both", "section", "group")]
    total = own.astype(F32)
    for other in others:
        total = total + other.astype(F32)
    total = after(total.astype(BF16), *gate2)
    return total, lax.ppermute(total, "mp", PAIR)


class Copies:
    def __init__(self, sems):
        self.sems, self.used, self.waits = sems, 0, []

    def start(self, pairs):
        for src, dst in pairs:
            copy = pltpu.make_async_copy(src, dst, self.sems.at[self.used])
            copy.start()
            self.waits.append(copy)
            self.used += 1

    def start_either(self, which, ifs, elses):
        first = self.used
        for holds, pairs in ((which, ifs), (jnp.logical_not(which), elses)):

            @pl.when(holds)
            def _():
                for k, (src, dst) in enumerate(pairs):
                    pltpu.make_async_copy(src, dst, self.sems.at[first + k]).start()

        for k, (src, dst) in enumerate(ifs):
            self.waits.append(pltpu.make_async_copy(src, dst, self.sems.at[first + k]))
        self.used += len(ifs)

    def wait(self):
        for copy in self.waits:
            copy.wait()
        self.waits = []


def rows_into(slot, dst, which=0):
    n, starts = dst.shape[0] // 8, []
    for ref in slot[:3]:
        starts += [(ref, which * n), (ref, ref.shape[0] // 2 + which * n)]
    starts += [(ref, 0) for ref in slot[3:]]
    return [(ref.at[pl.ds(at, n)], dst.at[pl.ds(k * n, n)]) for k, (ref, at) in enumerate(starts)]


def halves_into(mine, other, dst, core):
    half = mine.shape[1]
    return [
        (mine, dst.at[:, pl.ds(pl.multiple_of(core * half, half), half)]),
        (other, dst.at[:, pl.ds(pl.multiple_of((1 - core) * half, half), half)]),
    ]


def groups_into(own, other, dst, y):
    n = own.shape[0]
    return [
        (own, dst.at[pl.ds(pl.multiple_of(y * n, n), n)]),
        (other, dst.at[pl.ds(pl.multiple_of((1 - y) * n, n), n)]),
    ]


def write_part(adjoint, vs, keep, send, part, core):
    half = keep.shape[1]
    for k in range(2):
        part[k] = dot_t(adjoint[...], vs[k * half : (k + 1) * half, :])
    keep[...] = part[core]
    send[...] = part[1 - core]


def add_ranked(adjoint, rank, us, out, step):
    for at in range(0, adjoint.shape[1], step):
        columns = slice(at, at + step)
        delta = jnp.dot(rank[...], us[:, columns], preferred_element_type=F32)
        out[:, columns] = (adjoint[:, columns].astype(F32) + delta).astype(BF16)


def first_kernel(flags, g_own, g_other, *refs):
    slot1, slot2, (keep, send, g, vs, part, sems) = refs[:5], refs[5:10], refs[10:]
    last, y, core = flags[0] == 1, flags[1], flags[2]
    copies = Copies(sems)
    copies.start(groups_into(g_own, g_other, g, y))
    copies.start_either(last, rows_into(slot1, vs), rows_into(slot2, vs))
    copies.wait()
    write_part(g, vs, keep, send, part, core)


def middle_kernel(flags, g_own, g_other, mine, other, *refs):
    slot1, slot2, rest = refs[:5], refs[5:10], refs[10:15]
    adjoint, keep, send, g, rank, us, vs, part, sems = refs[15:]
    last, y, core = flags[0] == 1, flags[1], flags[2]
    copies = Copies(sems)
    copies.start(groups_into(g_own, g_other, g, y) + halves_into(mine, other, rank, core))
    copies.start_either(last, rows_into(slot2, us), rows_into(rest, us))
    copies.start_either(last, rows_into(rest, vs), rows_into(slot1, vs))
    copies.wait()
    add_ranked(g, rank, us, adjoint, 256)
    write_part(adjoint, vs, keep, send, part, core)


def last_kernel(flags, adjoint1, mine, other, *refs):
    rest, (here, to_x, to_xy, to_y, kept, rank, us, adjoint0, sems) = refs[:5], refs[5:]
    last, y, core = flags[0] == 1, flags[1], flags[2]
    n = here.shape[0]
    copies = Copies(sems)
    copies.start([(adjoint1, kept)] + halves_into(mine, other, rank, core))
    copies.start(rows_into(rest, us, 1))
    copies.wait()
    add_ranked(kept, rank, us, adjoint0, 256)

    def sends(own, others):
        return [
            (others.at[pl.ds(pl.multiple_of(y * n, n), n)], to_x),
            (others.at[pl.ds(pl.multiple_of((1 - y) * n, n), n)], to_xy),
            (own.at[pl.ds(pl.multiple_of((1 - y) * n, n), n)], to_y),
            (own.at[pl.ds(pl.multiple_of(y * n, n), n)], here),
        ]

    copies.start_either(last, sends(kept, adjoint0), sends(adjoint0, kept))
    copies.wait()


def score_kernel(shift, *refs):
    rows, (out, stacked) = refs[:-2], refs[-2:]
    n = rows[0].shape[0]
    for k, ref in enumerate(rows):
        stacked[k * n : (k + 1) * n, :] = ref[...].astype(F32)
    every = stacked[...].astype(BF16)
    kernel = dot_t(every, every)
    order = kernel.shape[0]
    row = lax.broadcasted_iota(jnp.int32, (order, order), 0)
    column = lax.broadcasted_iota(jnp.int32, (order, order), 1)
    left = kernel + jnp.where(row == column, shift[0], 0.0)
    right = kernel
    for k in range(order):
        inverse = 1.0 / left[k : k + 1, k : k + 1]
        left_row, right_row = left[k : k + 1, :] * inverse, right[k : k + 1, :] * inverse
        factor = left[:, k : k + 1]
        left = jnp.where(row == k, left_row, left - factor * left_row)
        right = jnp.where(row == k, right_row, right - factor * right_row)
    out[...] = jnp.sum(jnp.where(row == column, right, 0.0), axis=0, keepdims=True)


def scores_by_kernel(blocks, shift):
    order = len(blocks) * blocks[0].shape[0]
    return pl.pallas_call(
        score_kernel,
        name="scores",
        out_shape=jax.ShapeDtypeStruct((1, order), F32),
        in_specs=[pl.BlockSpec(memory_space=pltpu.SMEM)] + [pl.BlockSpec(memory_space=pltpu.VMEM)] * len(blocks),
        out_specs=pl.BlockSpec(memory_space=pltpu.VMEM),
        scratch_shapes=[pltpu.VMEM((order, blocks[0].shape[1]), F32)],
        compiler_params=pltpu.CompilerParams(vmem_limit_bytes=8 << 20),
    )(shift, *blocks)


def kernel_call(body, name, outs, scratch, copies, flags, *args):
    anywhere = pl.BlockSpec(memory_space=pl.ANY)
    return pl.pallas_call(
        body,
        name=name,
        out_shape=[o for o, _ in outs],
        in_specs=[pl.BlockSpec(memory_space=pltpu.SMEM)] + [anywhere] * len(args),
        out_specs=[anywhere if far else pl.BlockSpec(memory_space=pltpu.VMEM) for _, far in outs],
        scratch_shapes=[pltpu.VMEM(*shape) for shape in scratch] + [pltpu.SemaphoreType.DMA((copies,))],
        compiler_params=pltpu.CompilerParams(vmem_limit_bytes=16 << 20),
    )(flags, *[pltpu.with_memory_space_constraint(a, pltpu.HBM) if a.shape[1] > 512 else a for a in args])


def spread(acts, cotangent, in_weight, out_weight, in_factor, out_factor, damping, lengths):
    x, y, z = lax.axis_index("section"), lax.axis_index("group"), lax.axis_index("dp")
    tok_rows, width = cotangent.shape
    examples = lengths.shape[1]
    slice_width = width // 4

    def piece(a, px, py):
        return lax.dynamic_slice_in_dim(a, (px * 2 + py) * slice_width, slice_width, 1)

    v_own, u_own = out_weight[0], in_weight[0]
    last = x == 1

    n = v_own.shape[0]
    v_keep, u_keep = piece(v_own, x, y), piece(u_own, x, y)
    slot1 = gathered(v_keep, "slot1")
    v_other = lax.ppermute(piece(v_own, 1 - x, y), "section", PAIR)
    u_other = lax.ppermute(piece(u_own, 1 - x, y), "section", PAIR)
    g_own = piece(cotangent, x, y)
    g_other = lax.ppermute(piece(cotangent, x, 1 - y), "group", PAIR)
    slot2 = gathered(jnp.where(last, u_keep, v_other), "slot2")
    u_keep, v_other, u_other = after2((u_keep, v_other, u_other), *slot2[1:3], *slot1[3:])
    h = n // 2
    third, fourth = jnp.where(last, v_other, u_other), jnp.where(last, u_other, u_keep)
    both = jnp.concatenate([third[:h], fourth[:h], third[h:], fourth[h:]], 0)
    with jax.named_scope("slot34"):
        below, above = lax.ppermute(both, "dp", UP), lax.ppermute(both, "dp", DOWN)
    with jax.named_scope("slot3"):
        far3 = [lax.ppermute(below[:h], "dp", UP), lax.ppermute(above[n : n + h], "dp", DOWN)]
    with jax.named_scope("slot4"):
        ready = after2((below[h:n], above[n + h :]), *far3[:1])
        far4 = [lax.ppermute(ready[0], "dp", UP), lax.ppermute(ready[1], "dp", DOWN)]
    slot3, slot4 = [both, below, above, *far3], [both, below, above, *far4]

    flags = jnp.stack([x, y, lax.axis_index("mp")]).astype(jnp.int32)
    groups = lax.axis_size("group")
    ranks = 4 * n
    tokens = groups * tok_rows
    half_part = jax.ShapeDtypeStruct((tokens, ranks // 2), F32)
    shape_of = jax.ShapeDtypeStruct((tokens, slice_width), BF16)
    send_of = jax.ShapeDtypeStruct((tok_rows, slice_width), BF16)
    wide, rank_of = ((tokens, slice_width), BF16), ((tokens, ranks), BF16)
    weight, part_of = ((ranks, slice_width), BF16), ((2, tokens, ranks // 2), F32)

    keep, send = kernel_call(
        first_kernel, "first", [(half_part, False)] * 2, [wide, weight, part_of], 10, flags, g_own, g_other, *slot1, *slot2
    )
    mine1, other1 = summed(keep, send, F32, slot3[1:2], slot3[3:])
    adjoint1, keep, send = kernel_call(
        middle_kernel, "middle", [(shape_of, False), (half_part, False), (half_part, False)],
        [wide, rank_of, weight, weight, part_of], 20, flags, g_own, g_other, mine1, other1, *slot1, *slot2, *slot3,
    )
    mine0, other0 = summed(keep, send, BF16, (), slot4[3:])
    here, to_x, to_xy, to_y = kernel_call(
        last_kernel, "last", [(send_of, True)] * 4, [wide, rank_of, weight, wide], 15, flags, adjoint1, mine0, other0, *slot4
    )
    from_xy = lax.ppermute(to_xy, *plane("both"))
    from_x = lax.ppermute(to_x, *plane("section"))
    from_y = lax.ppermute(to_y, *plane("group"))

    def of_group(a, who):
        return lax.dynamic_slice_in_dim(a, who * tok_rows, tok_rows, 0)

    adjoint = jnp.zeros_like(cotangent)
    for value, px, py in ((here, x, y), (from_y, x, 1 - y), (from_x, 1 - x, y), (from_xy, 1 - x, 1 - y)):
        adjoint = lax.dynamic_update_slice_in_dim(adjoint, value, (px * 2 + py) * slice_width, 1)

    core = lax.axis_index("mp")
    mine, other = of_group(jnp.where(last, mine1, mine0), y), of_group(jnp.where(last, other1, other0), y)
    rank = jnp.where(core == 0, jnp.concatenate([mine, other], 1), jnp.concatenate([other, mine], 1))
    block = out_factor.shape[2] // 4
    factor = jnp.concatenate(
        [lax.dynamic_slice_in_dim(out_factor[0], lax.rem(z + k, 4) * block, block, 1) for k in (0, 3, 1, 2)], 1
    )
    out_proj = dot_t(rank, factor)
    in_part = dot_t(acts[0], in_factor[0])
    in_proj = in_part + lax.ppermute(in_part, "mp", PAIR)
    rows = own_rows(out_proj, in_proj, lengths[0])
    rows = after(rows, from_x)
    blocks = [rows] + [lax.ppermute(rows, "dp", p) for p in (UP, DOWN, OPPOSITE)]
    columns = rows.shape[1]
    scores = scores_by_kernel(blocks, damping * (columns * tok_rows / examples))[:, :examples]
    return (adjoint[None], scores)


def solution(mesh):
    sizes = (mesh.shape["group"], mesh.shape["dp"], mesh.shape["section"], mesh.shape["mp"])
    return jax.shard_map(
        spread if sizes == (2, 4, 2, 2) else relay,
        mesh=mesh,
        in_specs=(
            P("section", ("group", "dp"), "mp"),
            P(("group", "dp"), "mp"),
            P("section", "dp", "mp"),
            P("section", "dp", "mp"),
            P("section", None, "mp"),
            P("section", None, None),
            P("section"),
            P(("group", "dp"), None),
        ),
        out_specs=(P("section", ("group", "dp"), "mp"), P("section", ("group", "dp"))),
        check_vma=False,
    )
```

```python
import jax
import jax.numpy as jnp
from jax import lax
from jax.experimental import pallas as pl
from jax.experimental.pallas import tpu as pltpu
from jax.sharding import PartitionSpec as P

F32 = jnp.float32
BF16 = jnp.bfloat16
UP = ((0, 1), (1, 2), (2, 3), (3, 0))
DOWN = ((1, 0), (2, 1), (3, 2), (0, 3))
OPPOSITE = ((0, 2), (2, 0), (1, 3), (3, 1))
ACROSS = ((0, 3), (3, 0), (1, 2), (2, 1))
PAIR = ((0, 1), (1, 0))


def dot_t(a, b, **kw):
    return lax.dot_general(a, b, (((1,), (1,)), ((), ())), preferred_element_type=F32, **kw)


def after(x, *first):
    return lax.optimization_barrier((x, *first))[0]


def after2(xs, *first):
    return lax.optimization_barrier((*xs, *first))[: len(xs)]


def shifted(shard, axis, by):
    devices = lax.axis_size(axis)
    pairs = [(i, i + by) for i in range(devices) if 0 <= i + by < devices]
    return lax.ppermute(shard, axis, pairs)


def member_of(lengths, tok_rows):
    examples = lengths.shape[0]
    upto = jnp.arange(examples)[:, None] <= jnp.arange(examples)[None, :]
    ends = jnp.sum(jnp.where(upto, lengths[:, None], 0), axis=0)
    positions = jnp.arange(tok_rows, dtype=jnp.int32)
    doc_index = jnp.sum((positions[:, None] >= ends[None, :]).astype(jnp.int32), axis=1)
    return (doc_index[:, None] == jnp.arange(examples, dtype=jnp.int32)[None, :]).astype(F32)


def own_rows(out_proj, in_proj, lengths):
    member = member_of(lengths, out_proj.shape[0])
    rows = jnp.einsum("te,to,ti->eoi", member, out_proj, in_proj, precision=lax.Precision.HIGHEST)
    return rows.reshape(lengths.shape[0], -1).astype(BF16)


def scores_of(every_row, damping, start, examples, tok_rows):
    columns = every_row.shape[1]
    kernel = dot_t(every_row, every_row)
    shift_value = damping * (columns * tok_rows / examples)
    factor = jnp.linalg.cholesky(kernel + shift_value * jnp.eye(kernel.shape[0], dtype=F32))
    own_columns = lax.dynamic_slice_in_dim(kernel, start, examples, 1)
    first = lax.linalg.triangular_solve(factor, own_columns, left_side=True, lower=True)
    second = lax.linalg.triangular_solve(factor, first, left_side=True, lower=True, transpose_a=True)
    own_block = lax.dynamic_slice_in_dim(second, start, examples, 0)
    return jnp.sum(own_block * jnp.eye(examples, dtype=F32), axis=1)


def relay(acts, cotangent, in_weight, out_weight, in_factor, out_factor, damping, lengths):
    sections = lax.axis_size("section")
    section_index = lax.axis_index("section")
    tok_rows = cotangent.shape[0]
    examples = lengths.shape[1]
    u_full = lax.all_gather(in_weight[0], "dp", axis=0, tiled=True)
    v_full = lax.all_gather(out_weight[0], "dp", axis=0, tiled=True)
    adjoint_now = cotangent
    kept_rank = jnp.zeros((tok_rows, v_full.shape[0]), BF16)
    kept_adjoint = jnp.zeros_like(cotangent)
    for turn in range(sections):
        partial_rank = dot_t(adjoint_now, v_full)
        own_half = lax.psum_scatter(partial_rank, "mp", scatter_dimension=1, tiled=True).astype(BF16)
        rank_grad = lax.all_gather(own_half, "mp", axis=1, tiled=True)
        new_adjoint = (
            adjoint_now.astype(F32) + jnp.dot(rank_grad, u_full, preferred_element_type=F32)
        ).astype(BF16)
        active = section_index == sections - 1 - turn
        kept_rank = jnp.where(active, rank_grad, kept_rank)
        kept_adjoint = jnp.where(active, new_adjoint, kept_adjoint)
        if turn + 1 < sections:
            adjoint_now = shifted(new_adjoint, "section", -1)
    out_proj = dot_t(kept_rank, out_factor[0])
    in_proj = lax.psum(dot_t(acts[0], in_factor[0]), "mp")
    rows = own_rows(out_proj, in_proj, lengths[0])
    every_row = lax.all_gather(rows, "dp", axis=0, tiled=True)
    start = lax.axis_index("dp") * examples
    scores = scores_of(every_row, damping[0], start, examples, tok_rows)
    return (kept_adjoint[None], scores[None])


def gathered(w, name):
    half = w.shape[0] // 2
    with jax.named_scope(name):
        below, above = lax.ppermute(w, "dp", UP), lax.ppermute(w, "dp", DOWN)
        upper, lower = lax.ppermute(below[:half], "dp", UP), lax.ppermute(above[half:], "dp", DOWN)
    return [w, below, above, upper, lower]


def plane(axis):
    return (axis, PAIR) if axis != "both" else (("group", "section"), ACROSS)


def summed(keep, send, gate1, gate2):
    own = after((keep + lax.ppermute(send, "mp", PAIR)).astype(BF16), *gate1)
    others = [lax.ppermute(own, *plane(a)) for a in ("both", "section", "group")]
    total = own.astype(F32)
    for other in others:
        total = total + other.astype(F32)
    total = after(total.astype(BF16), *gate2)
    return total, lax.ppermute(total, "mp", PAIR)


class Copies:
    def __init__(self, sems):
        self.sems, self.used, self.waits = sems, 0, []

    def start(self, pairs):
        for src, dst in pairs:
            copy = pltpu.make_async_copy(src, dst, self.sems.at[self.used])
            copy.start()
            self.waits.append(copy)
            self.used += 1

    def start_either(self, which, ifs, elses):
        first = self.used
        for holds, pairs in ((which, ifs), (jnp.logical_not(which), elses)):

            @pl.when(holds)
            def _():
                for k, (src, dst) in enumerate(pairs):
                    pltpu.make_async_copy(src, dst, self.sems.at[first + k]).start()

        for k, (src, dst) in enumerate(ifs):
            self.waits.append(pltpu.make_async_copy(src, dst, self.sems.at[first + k]))
        self.used += len(ifs)

    def wait(self):
        for copy in self.waits:
            copy.wait()
        self.waits = []


def rows_into(slot, dst, which=0):
    n, starts = dst.shape[0] // 8, []
    for ref in slot[:3]:
        starts += [(ref, which * n), (ref, ref.shape[0] // 2 + which * n)]
    starts += [(ref, 0) for ref in slot[3:]]
    return [(ref.at[pl.ds(at, n)], dst.at[pl.ds(k * n, n)]) for k, (ref, at) in enumerate(starts)]


def halves_into(mine, other, dst, core):
    half = mine.shape[1]
    return [
        (mine, dst.at[:, pl.ds(pl.multiple_of(core * half, half), half)]),
        (other, dst.at[:, pl.ds(pl.multiple_of((1 - core) * half, half), half)]),
    ]


def groups_into(own, other, dst, y):
    n = own.shape[0]
    return [
        (own, dst.at[pl.ds(pl.multiple_of(y * n, n), n)]),
        (other, dst.at[pl.ds(pl.multiple_of((1 - y) * n, n), n)]),
    ]


def write_part(adjoint, vs, keep, send, part, core):
    half = keep.shape[1]
    for k in range(2):
        part[k] = dot_t(adjoint[...], vs[k * half : (k + 1) * half, :])
    keep[...] = part[core]
    send[...] = part[1 - core]


def add_ranked(adjoint, rank, us, out, step):
    for at in range(0, adjoint.shape[1], step):
        columns = slice(at, at + step)
        delta = jnp.dot(rank[...], us[:, columns], preferred_element_type=F32)
        out[:, columns] = (adjoint[:, columns].astype(F32) + delta).astype(BF16)


def first_kernel(flags, g_own, g_other, *refs):
    slot1, slot2, (keep, send, g, vs, part, sems) = refs[:5], refs[5:10], refs[10:]
    last, y, core = flags[0] == 1, flags[1], flags[2]
    copies = Copies(sems)
    copies.start(groups_into(g_own, g_other, g, y))
    copies.start_either(last, rows_into(slot1, vs), rows_into(slot2, vs))
    copies.wait()
    write_part(g, vs, keep, send, part, core)


def middle_kernel(flags, g_own, g_other, mine, other, *refs):
    slot1, slot2, rest = refs[:5], refs[5:10], refs[10:15]
    adjoint, keep, send, g, rank, us, vs, part, sems = refs[15:]
    last, y, core = flags[0] == 1, flags[1], flags[2]
    copies = Copies(sems)
    copies.start(groups_into(g_own, g_other, g, y) + halves_into(mine, other, rank, core))
    copies.start_either(last, rows_into(slot2, us), rows_into(rest, us))
    copies.start_either(last, rows_into(rest, vs), rows_into(slot1, vs))
    copies.wait()
    add_ranked(g, rank, us, adjoint, 256)
    write_part(adjoint, vs, keep, send, part, core)


def last_kernel(flags, adjoint1, mine, other, *refs):
    rest, (here, to_x, to_xy, to_y, kept, rank, us, adjoint0, sems) = refs[:5], refs[5:]
    last, y, core = flags[0] == 1, flags[1], flags[2]
    n = here.shape[0]
    copies = Copies(sems)
    copies.start([(adjoint1, kept)] + halves_into(mine, other, rank, core))
    copies.start(rows_into(rest, us, 1))
    copies.wait()
    add_ranked(kept, rank, us, adjoint0, 256)

    def sends(own, others):
        return [
            (others.at[pl.ds(pl.multiple_of(y * n, n), n)], to_x),
            (others.at[pl.ds(pl.multiple_of((1 - y) * n, n), n)], to_xy),
            (own.at[pl.ds(pl.multiple_of((1 - y) * n, n), n)], to_y),
            (own.at[pl.ds(pl.multiple_of(y * n, n), n)], here),
        ]

    copies.start_either(last, sends(kept, adjoint0), sends(adjoint0, kept))
    copies.wait()


def score_kernel(shift, *refs):
    rows, (out, stacked) = refs[:-2], refs[-2:]
    n = rows[0].shape[0]
    for k, ref in enumerate(rows):
        stacked[k * n : (k + 1) * n, :] = ref[...].astype(F32)
    every = stacked[...].astype(BF16)
    kernel = dot_t(every, every)
    order = kernel.shape[0]
    row = lax.broadcasted_iota(jnp.int32, (order, order), 0)
    column = lax.broadcasted_iota(jnp.int32, (order, order), 1)
    left = kernel + jnp.where(row == column, shift[0], 0.0)
    right = kernel
    for k in range(order):
        inverse = 1.0 / left[k : k + 1, k : k + 1]
        left_row, right_row = left[k : k + 1, :] * inverse, right[k : k + 1, :] * inverse
        factor = left[:, k : k + 1]
        left = jnp.where(row == k, left_row, left - factor * left_row)
        right = jnp.where(row == k, right_row, right - factor * right_row)
    out[...] = jnp.sum(jnp.where(row == column, right, 0.0), axis=0, keepdims=True)


def scores_by_kernel(blocks, shift):
    order = len(blocks) * blocks[0].shape[0]
    return pl.pallas_call(
        score_kernel,
        name="scores",
        out_shape=jax.ShapeDtypeStruct((1, order), F32),
        in_specs=[pl.BlockSpec(memory_space=pltpu.SMEM)] + [pl.BlockSpec(memory_space=pltpu.VMEM)] * len(blocks),
        out_specs=pl.BlockSpec(memory_space=pltpu.VMEM),
        scratch_shapes=[pltpu.VMEM((order, blocks[0].shape[1]), F32)],
        compiler_params=pltpu.CompilerParams(vmem_limit_bytes=8 << 20),
    )(shift, *blocks)


def kernel_call(body, name, outs, scratch, copies, flags, *args):
    anywhere = pl.BlockSpec(memory_space=pl.ANY)
    return pl.pallas_call(
        body,
        name=name,
        out_shape=[o for o, _ in outs],
        in_specs=[pl.BlockSpec(memory_space=pltpu.SMEM)] + [anywhere] * len(args),
        out_specs=[anywhere if far else pl.BlockSpec(memory_space=pltpu.VMEM) for _, far in outs],
        scratch_shapes=[pltpu.VMEM(*shape) for shape in scratch] + [pltpu.SemaphoreType.DMA((copies,))],
        compiler_params=pltpu.CompilerParams(vmem_limit_bytes=16 << 20),
    )(flags, *[pltpu.with_memory_space_constraint(a, pltpu.HBM) if a.shape[1] > 512 else a for a in args])


def spread(acts, cotangent, in_weight, out_weight, in_factor, out_factor, damping, lengths):
    x, y, z = lax.axis_index("section"), lax.axis_index("group"), lax.axis_index("dp")
    tok_rows, width = cotangent.shape
    examples = lengths.shape[1]
    slice_width = width // 4

    def piece(a, px, py):
        return lax.dynamic_slice_in_dim(a, (px * 2 + py) * slice_width, slice_width, 1)

    v_own, u_own = out_weight[0], in_weight[0]
    last = x == 1

    n = v_own.shape[0]
    v_keep, u_keep = piece(v_own, x, y), piece(u_own, x, y)
    slot1 = gathered(v_keep, "slot1")
    v_other = lax.ppermute(piece(v_own, 1 - x, y), "section", PAIR)
    u_other = lax.ppermute(piece(u_own, 1 - x, y), "section", PAIR)
    g_own = piece(cotangent, x, y)
    g_other = lax.ppermute(piece(cotangent, x, 1 - y), "group", PAIR)
    slot2 = gathered(jnp.where(last, u_keep, v_other), "slot2")
    u_keep, v_other, u_other = after2((u_keep, v_other, u_other), *slot2[1:3])
    h = n // 2
    third, fourth = jnp.where(last, v_other, u_other), jnp.where(last, u_other, u_keep)
    both = jnp.concatenate([third[:h], fourth[:h], third[h:], fourth[h:]], 0)
    with jax.named_scope("slot34"):
        below, above = lax.ppermute(both, "dp", UP), lax.ppermute(both, "dp", DOWN)
    with jax.named_scope("slot3"):
        far3 = [lax.ppermute(below[:h], "dp", UP), lax.ppermute(above[n : n + h], "dp", DOWN)]
    with jax.named_scope("slot4"):
        ready = after2((below[h:n], above[n + h :]), *far3[:1])
        far4 = [lax.ppermute(ready[0], "dp", UP), lax.ppermute(ready[1], "dp", DOWN)]
    slot3, slot4 = [both, below, above, *far3], [both, below, above, *far4]

    flags = jnp.stack([x, y, lax.axis_index("mp")]).astype(jnp.int32)
    groups = lax.axis_size("group")
    ranks = 4 * n
    tokens = groups * tok_rows
    half_part = jax.ShapeDtypeStruct((tokens, ranks // 2), F32)
    shape_of = jax.ShapeDtypeStruct((tokens, slice_width), BF16)
    send_of = jax.ShapeDtypeStruct((tok_rows, slice_width), BF16)
    wide, rank_of = ((tokens, slice_width), BF16), ((tokens, ranks), BF16)
    weight, part_of = ((ranks, slice_width), BF16), ((2, tokens, ranks // 2), F32)

    keep, send = kernel_call(
        first_kernel, "first", [(half_part, False)] * 2, [wide, weight, part_of], 10, flags, g_own, g_other, *slot1, *slot2
    )
    mine1, other1 = summed(keep, send, slot3[1:2], slot3[3:])
    adjoint1, keep, send = kernel_call(
        middle_kernel, "middle", [(shape_of, False), (half_part, False), (half_part, False)],
        [wide, rank_of, weight, weight, part_of], 20, flags, g_own, g_other, mine1, other1, *slot1, *slot2, *slot3,
    )
    mine0, other0 = summed(keep, send, (), slot4[3:])
    here, to_x, to_xy, to_y = kernel_call(
        last_kernel, "last", [(send_of, True)] * 4, [wide, rank_of, weight, wide], 15, flags, adjoint1, mine0, other0, *slot4
    )
    from_xy = lax.ppermute(to_xy, *plane("both"))
    from_x = lax.ppermute(to_x, *plane("section"))
    from_y = lax.ppermute(to_y, *plane("group"))

    def of_group(a, who):
        return lax.dynamic_slice_in_dim(a, who * tok_rows, tok_rows, 0)

    adjoint = jnp.zeros_like(cotangent)
    for value, px, py in ((here, x, y), (from_y, x, 1 - y), (from_x, 1 - x, y), (from_xy, 1 - x, 1 - y)):
        adjoint = lax.dynamic_update_slice_in_dim(adjoint, value, (px * 2 + py) * slice_width, 1)

    core = lax.axis_index("mp")
    mine, other = of_group(jnp.where(last, mine1, mine0), y), of_group(jnp.where(last, other1, other0), y)
    rank = jnp.where(core == 0, jnp.concatenate([mine, other], 1), jnp.concatenate([other, mine], 1))
    block = out_factor.shape[2] // 4
    factor = jnp.concatenate(
        [lax.dynamic_slice_in_dim(out_factor[0], lax.rem(z + k, 4) * block, block, 1) for k in (0, 3, 1, 2)], 1
    )
    out_proj = dot_t(rank, factor)
    in_part = dot_t(acts[0], in_factor[0])
    in_proj = in_part + lax.ppermute(in_part, "mp", PAIR)
    rows = own_rows(out_proj, in_proj, lengths[0])
    rows = after(rows, from_x)
    split = [(2 * a, 2 * b) for a, b in UP] + [(2 * a + 1, 2 * b + 1) for a, b in DOWN]
    near = lax.ppermute(rows, ("dp", "mp"), split)
    across = lax.ppermute(rows, "dp", OPPOSITE)
    swapped = lax.ppermute(near, "mp", PAIR)
    blocks = [rows, jnp.where(core == 0, near, swapped), jnp.where(core == 0, swapped, near), across]
    columns = rows.shape[1]
    scores = scores_by_kernel(blocks, damping * (columns * tok_rows / examples))[:, :examples]
    return (adjoint[None], scores)


def solution(mesh):
    sizes = (mesh.shape["group"], mesh.shape["dp"], mesh.shape["section"], mesh.shape["mp"])
    return jax.shard_map(
        spread if sizes == (2, 4, 2, 2) else relay,
        mesh=mesh,
        in_specs=(
            P("section", ("group", "dp"), "mp"),
            P(("group", "dp"), "mp"),
            P("section", "dp", "mp"),
            P("section", "dp", "mp"),
            P("section", None, "mp"),
            P("section", None, None),
            P("section"),
            P(("group", "dp"), None),
        ),
        out_specs=(P("section", ("group", "dp"), "mp"), P("section", ("group", "dp"))),
        check_vma=False,
    )
```
